512 devices in a mesh: contact: 8 (over x, core), body: 8 (over z), group: 8 (over y).
Axes of the slice: x: 4, y: 8, z: 8, core: 2. Of those that a mesh axis runs over, the one named last changes fastest.
Arguments:
- jacobian_a: float32 [18, 1835008], P(None, ('contact', 'body', 'group')), may hold values from -4 to 4
- jacobian_b: float32 [18, 1835008], P(None, ('contact', 'body', 'group')), may hold values from -4 to 4
- warm_start: float32 [3, 1835008], P(None, ('contact', 'body', 'group')), may hold values from -4 to 4
- free_gap: float32 [3, 1835008], P(None, ('contact', 'body', 'group')), may hold values from -25 to 25
- compliance: float32 [3, 1835008], P(None, ('contact', 'body', 'group')), may hold values from 0.05 to 2.5
- friction: float32 [1835008], P(('contact', 'body', 'group')), may hold values from 0.2 to 0.8
- cone_active: int32 [1835008], P(('contact', 'body', 'group')), may hold values 0 or 1
- body_index_a: int32 [1835008], P(('contact', 'body', 'group')), may hold values from 0 to 4095
- body_index_b: int32 [1835008], P(('contact', 'body', 'group')), may hold values from 0 to 4095
- block_owner: int32 [28672, 1], P(('contact', 'body', 'group')), may hold values from 0 to 63; in each aligned block of 56 rows (0 to 55, 56 to 111, ...) at most 2 rows name the same one
- inverse_mass: float32 [6, 262144], P(None, ('body', 'group')), may hold values from 0.3 to 3
- free_velocity: float32 [6, 262144], P(None, ('body', 'group')), may hold values from -6 to 6
Outputs:
- impulse: float32 [3, 1835008], P(None, ('contact', 'body', 'group'))
- velocity: float32 [6, 262144], P(None, ('body', 'group'))
The draws below stay inside these ranges and needn't reach their ends.
Inputs may be any that keep to these rules, and one draw needn't show every extreme that they name: `block_owner`: in each aligned block of 56 rows (the contact blocks of one device) no shard is named more than 2 times.
All inputs are finite; a program needn't handle non-finite values. No bound on the sum of `cone_active` on one device may be relied on, other than what follows from the above.
Results may differ from the reference program's by a relative error of at most 0.0003.
Values sent between devices are 32-bit elements; how exact they have to be, the bound alone decides.
A program may use at most 64 MiB of HBM per device.

```python
import math
import jax
import jax.numpy as jnp
import numpy as np
from jax import lax

NBLK = 56
CBLK = 64
BOD_DEV = 4096
ITERS = 2
SHARDS = 64
CAP = 2
CON_DEV = 3584
CONTACTS = 1835008
BLOCKS = 28672
BODIES = 262144
N_BODY = 8
N_GROUP = 8


def draw_free_gap(key, part):
    key = jax.random.fold_in(key, 11)
    noise_key, scale_key = jax.random.split(key)
    position = jnp.arange(CONTACTS, dtype=jnp.float32) / CONTACTS
    spread = jnp.exp(jax.random.uniform(scale_key, (CONTACTS,), jnp.float32) * math.log(10.0))
    baseline = jnp.clip(jax.random.normal(noise_key, (3, CONTACTS), jnp.float32), -4.0, 4.0)
    trend_factor = 1.0 + 2.0 * position
    return 0.12 * baseline * spread[None, :] * trend_factor[None, :]


def draw_compliance(key, part):
    key = jax.random.fold_in(key, 23)
    position = jnp.arange(CONTACTS, dtype=jnp.float32) / CONTACTS
    baseline = 0.05 * jnp.exp(jax.random.uniform(key, (3, CONTACTS), jnp.float32) * math.log(10.0))
    trend_factor = 3.0 - 2.0 * position
    return baseline * trend_factor[None, :]


def with_ends(values, own_key, smallest, largest):
    place = [jax.random.randint(jax.random.fold_in(own_key, axis), (), 0, length) for axis, length in enumerate(values.shape)]
    main_axis = values.shape.index(max(values.shape))
    beside = place[:main_axis] + [(place[main_axis] + 1) % values.shape[main_axis]] + place[main_axis + 1:]
    return values.at[tuple(place)].set(smallest).at[tuple(beside)].set(largest)


def steps_of(rng, dims, cuts, least, high):
    def one(axis_at, shards_of):
        draws = jax.random.uniform(jax.random.fold_in(jax.random.fold_in(rng, 6), axis_at), (shards_of,), jnp.float32, least / len(cuts), high / len(cuts))
        return jnp.repeat(jnp.exp(draws), dims[axis_at] // shards_of).reshape((-1,) + (1,) * (len(dims) - axis_at - 1))

    level = one(*cuts[0])
    for cut in cuts[1:]:
        level = level * one(*cut)
    return level


def shared_out(rng, own, number, rows, amount, top, reach, slope):
    ranking = jax.random.permutation(rng, amount)
    packed, usual = shares(amount, rows * top, reach, slope, True), shares(amount, rows * top, reach, slope, False)
    places = jnp.arange(amount)

    def named(tallies, offset_by):
        used = int((tallies > 0).sum())
        fixed = max(1, used // 4)
        shifted = fixed + (places - fixed + offset_by * (used - fixed)) % max(1, amount - fixed)
        return jnp.zeros((amount,), jnp.int32).at[ranking[jnp.where(places < fixed, places, shifted)]].set(jnp.asarray(tallies, jnp.int32))

    tallies = jnp.where(number % 4 == 0, named(packed, number // 4), named(usual, number - number // 4 - 1))
    mixed = jax.random.permutation(jax.random.fold_in(own, 3), amount)
    donor, sink = mixed[0:amount // 2 * 2:2], mixed[1:amount // 2 * 2:2]
    margin = jnp.minimum(tallies[donor] - 1, reach - tallies[sink]) // 2
    margin = jnp.where((donor == ranking[0]) | (sink == ranking[0]) | (tallies[sink] == 0), 0, jnp.maximum(margin, 0))
    shifted = jax.random.randint(jax.random.fold_in(own, 4), (amount // 2,), 0, 1 << 20) % (margin + 1)
    tallies = tallies.at[donor].add(-shifted).at[sink].add(shifted)
    items = jnp.searchsorted(jnp.cumsum(tallies), jnp.arange(rows * top), side="right").astype(jnp.int32)
    listing = items.reshape(top, rows).T
    listing = listing[jax.random.permutation(jax.random.fold_in(own, 1), rows)]
    offset_by = jax.random.randint(jax.random.fold_in(own, 2), (rows, 1), 0, top)
    return jnp.take_along_axis(listing, (jnp.arange(top)[None, :] + offset_by) % top, axis=1)


def shares(number_of, total, reach, lean, full):
    loads = [(1 << 20) // math.isqrt(grade ** lean) + 1 for grade in range(1, number_of + 1)]
    largest = reach if full else min(reach, max(-(-total // number_of), total * loads[0] // sum(loads)))
    least = 1 if total - largest >= number_of - 1 else 0
    holding, spare = [largest] + [least] * (number_of - 1), total - largest - least * (number_of - 1)
    while spare > 0:
        free = [i for i in range(1, number_of) if holding[i] < largest] or [i for i in range(1, number_of) if holding[i] < reach]
        pool, budget = sum([loads[i] for i in free]), spare
        for i in free:
            addition = min(reach - holding[i], max(1, budget * loads[i] // pool), spare)
            holding[i] = holding[i] + addition
            spare = spare - addition
    return np.array(holding)


def scatter_about(own_key, extent, width, limit, cuts=(), kind=jnp.bfloat16):
    drawn = jax.random.normal(own_key, extent, jnp.float32) * width
    if len(cuts) > 0:
        drawn = steps_of(own_key, extent, cuts, -0.22, 0.18) * drawn
    return jnp.clip(drawn, min=-limit, max=limit).astype(kind)


def setup_inputs(seed: int = 0) -> dict:
    key_of = jax.random.split(jax.random.key(seed), 13)
    jacobian_a = scatter_about(key_of[0], (18, CONTACTS), 0.25, 4.0, ((1, 512),), jnp.float32)
    jacobian_b = scatter_about(key_of[1], (18, CONTACTS), 0.25, 4.0, ((1, 512),), jnp.float32)
    warm_start = scatter_about(key_of[2], (3, CONTACTS), 0.5, 4.0, ((1, 512),), jnp.float32)
    free_gap = draw_free_gap(jax.random.fold_in(key_of[12], 71), 0)
    compliance = draw_compliance(jax.random.fold_in(key_of[12], 71), 0)
    friction = jnp.clip(0.2 + 0.6 * jax.random.uniform(key_of[5], (CONTACTS,), jnp.float32) ** steps_of(key_of[5], (CONTACTS,), ((0, 512),), -0.2, 0.2), 0.2, 0.8)
    cone_active = with_ends((jax.random.randint(key_of[6], (CONTACTS,), 0, 4) < 3).astype(jnp.int32), jax.random.fold_in(key_of[6], 1), 0, 1)
    body_index_a = with_ends(jax.random.randint(key_of[7], (CONTACTS,), 0, BOD_DEV), jax.random.fold_in(key_of[7], 1), 0, BOD_DEV - 1).astype(jnp.int32)
    body_index_b = with_ends(jax.random.randint(key_of[8], (CONTACTS,), 0, BOD_DEV), jax.random.fold_in(key_of[8], 1), 0, BOD_DEV - 1).astype(jnp.int32)
    block_owner_keys = jax.random.split(jax.random.fold_in(key_of[9], 1), BLOCKS // NBLK)
    block_owner_turns = jax.random.permutation(jax.random.fold_in(key_of[9], 3), BLOCKS // NBLK)
    block_owner = jax.vmap(lambda own, number: shared_out(jax.random.fold_in(key_of[9], 2), own, number, NBLK, SHARDS, 1, CAP, 1))(block_owner_keys, block_owner_turns).reshape((BLOCKS, 1))
    inverse_mass = jnp.clip(jnp.exp(math.log(3.0) - 2.3025851 * jax.random.uniform(key_of[10], (6, BODIES), jnp.float32) ** steps_of(key_of[10], (6, BODIES), ((1, 64),), -0.2, 0.2)), 0.3, 3.0)
    free_velocity = scatter_about(key_of[11], (6, BODIES), 1.0, 6.0, ((1, 64),), jnp.float32)
    return {"jacobian_a": jacobian_a, "jacobian_b": jacobian_b, "warm_start": warm_start, "free_gap": free_gap, "compliance": compliance, "friction": friction, "cone_active": cone_active, "body_index_a": body_index_a, "body_index_b": body_index_b, "block_owner": block_owner, "inverse_mass": inverse_mass, "free_velocity": free_velocity}


EPS = 1e-06
SMOOTH = 0.1

def momentum_table(iterations):
    theta_now = 1.0
    coefficients = []
    for rounds in range(iterations):
        following = 0.5 * (theta_now * math.sqrt(theta_now * theta_now + 4.0) - theta_now * theta_now)
        coefficients.append(theta_now * (1.0 - theta_now) / (theta_now * theta_now + following))
        theta_now = following
    return coefficients

def project_cone(values, friction, cone_active):
    normal = values[0]
    tangent = values[1:3]
    spread = jnp.sqrt(tangent[0] * tangent[0] + tangent[1] * tangent[1] + SMOOTH * SMOOTH)
    sticking = spread <= friction * normal
    separated = friction * spread <= -normal
    cone_normal = (normal + friction * spread) / (1.0 + friction * friction)
    shrink_factor = friction * cone_normal / spread
    new_normal = jnp.where(sticking, normal, jnp.where(separated, 0.0, cone_normal))
    new_tangent = jnp.where(sticking[None], tangent, jnp.where(separated[None], 0.0, shrink_factor[None] * tangent))
    switched = cone_active == 1
    out_normal = jnp.where(switched, new_normal, jnp.maximum(normal, 0.0))
    out_tangent = jnp.where(switched[None], new_tangent, 0.0)
    return jnp.concatenate([out_normal[None], out_tangent], axis=0)

def impulse_terms(jacobian, values):
    return lax.optimization_barrier(jnp.sum(jacobian.reshape(3, 6, -1) * values[:, None, :], axis=0))

def velocity_terms(jacobian, velocities):
    return lax.optimization_barrier(jnp.sum(jacobian.reshape(3, 6, -1) * velocities[None, :, :], axis=1))

def reference(jacobian_a, jacobian_b, warm_start, free_gap, compliance, friction, cone_active, body_index_a, body_index_b, block_owner, inverse_mass, free_velocity):
    contact_ids = jnp.arange(body_index_a.shape[0], dtype=jnp.int32)
    home_shard = contact_ids // CON_DEV % (N_BODY * N_GROUP)
    body_a = (home_shard * BOD_DEV + body_index_a).astype(jnp.int32)
    body_b = (jnp.repeat(block_owner[:, 0], CBLK) * BOD_DEV + body_index_b).astype(jnp.int32)
    total_bodies = inverse_mass.shape[1]

    def body_impulse(values):
        summed = jnp.zeros((6, total_bodies), jnp.float32)
        summed = summed.at[:, body_a].add(impulse_terms(jacobian_a, values))
        return summed.at[:, body_b].add(impulse_terms(jacobian_b, values))

    def operator(values):
        moving = inverse_mass * body_impulse(values)
        return velocity_terms(jacobian_a, moving[:, body_a]) + velocity_terms(jacobian_b, moving[:, body_b]) + compliance * values
    momentum = momentum_table(ITERS)
    current = warm_start
    before = jnp.zeros_like(warm_start)
    gradient_before = free_gap
    latest = warm_start
    for rounds in range(ITERS):
        gradient = operator(current) + free_gap
        iterate_change = current - before
        gradient_change = gradient - gradient_before
        change_squares = jnp.sum(iterate_change * iterate_change)
        gradient_squares = jnp.sum(gradient_change * gradient_change)
        stride = jnp.sqrt((change_squares + EPS) / (gradient_squares + EPS))
        projected = project_cone(current - stride * gradient, friction, cone_active)
        following = projected + momentum[rounds] * (projected - latest)
        before, gradient_before, latest, current = (current, gradient, projected, following)
    velocity = free_velocity + inverse_mass * body_impulse(latest)
    return (latest, velocity)
```

```python
import math

import jax
import jax.numpy as jnp
from jax import lax
from jax.experimental import pallas as pl
from jax.experimental.pallas import tpu as pltpu
from jax.sharding import Mesh
from jax.sharding import PartitionSpec as P

CBLK = 64
ITERS = 2
CONTACT = ("contact_0", "contact_1")
SHARD = ("body", "group")
CONTACT_BODY_GROUP = ("contact_0", "contact_1", "body", "group")

EPS = 1e-06
SMOOTH = 0.1

LANES = 256
ROWS = 16
CHUNK = 512
WIDE = CHUNK // 128

VMEM = pl.BlockSpec(memory_space=pltpu.VMEM)
SMEM = pl.BlockSpec(memory_space=pltpu.SMEM)


def momentum_table(iterations):
    theta_now = 1.0
    coefficients = []
    for rounds in range(iterations):
        following = 0.5 * (
            theta_now * math.sqrt(theta_now * theta_now + 4.0) - theta_now * theta_now
        )
        coefficients.append(theta_now * (1.0 - theta_now) / (theta_now * theta_now + following))
        theta_now = following
    return coefficients


def slot_places(block_owner, capacity):
    target = block_owner[:, 0]
    matching = (target[:, None] == target[None, :]).astype(jnp.int32)
    ordinal = jnp.arange(target.shape[0], dtype=jnp.int32)
    earlier = (ordinal[None, :] < ordinal[:, None]).astype(jnp.int32)
    ranking = jnp.sum(matching * earlier, axis=1)
    return target * capacity + ranking


def exchange(array, axes):
    return lax.all_to_all(array, axes, 0, 0, tiled=True)


def impulse_rows(jacobian, values):
    total = jacobian[0:6] * values[0:1]
    for r in range(1, 3):
        total = total + jacobian[6 * r : 6 * r + 6] * values[r : r + 1]
    return total


def velocity_rows(jacobian, velocities):
    rows = [
        jnp.sum(jacobian[6 * r : 6 * r + 6] * velocities, axis=0, keepdims=True)
        for r in range(3)
    ]
    return jnp.concatenate(rows, axis=0)


def lane_onehot(index):
    lane = index & (LANES - 1)
    iota = lax.broadcasted_iota(jnp.int32, (LANES, index.shape[1]), 0)
    return jnp.where(iota == lane, 1.0, 0.0).astype(jnp.bfloat16)


def row_mask(index):
    iota = lax.broadcasted_iota(jnp.int32, (ROWS, index.shape[1]), 0)
    return iota == (index >> 8)


def pair(values):
    high = values.astype(jnp.bfloat16).astype(jnp.float32)
    return high, values - high


def scatter_chunk(acc_ref, terms, index):
    mask = row_mask(index)
    high, low = pair(terms)
    parts = [jnp.where(mask, part[c : c + 1], 0.0) for part in (high, low) for c in range(6)]
    spread = jnp.concatenate(parts, axis=0).astype(jnp.bfloat16)
    acc_ref[...] += lax.dot_general(
        spread,
        lane_onehot(index),
        (((1,), (1,)), ((), ())),
        preferred_element_type=jnp.float32,
    )


def gather_chunk(table, index):
    mask = row_mask(index)
    found = jnp.dot(table, lane_onehot(index), preferred_element_type=jnp.float32)
    found = found[: 6 * ROWS] + found[6 * ROWS :]
    rows = [
        jnp.sum(jnp.where(mask, found[ROWS * c : ROWS * (c + 1)], 0.0), axis=0, keepdims=True)
        for c in range(6)
    ]
    return rows


def pack_rows(places_ref, packed, out_ref):
    out_ref[...] = jnp.zeros_like(out_ref)
    lane = lax.broadcasted_iota(jnp.int32, (8, 128), 1)
    for i in range(packed.shape[1] // 128):
        tile = packed[:, 128 * i : 128 * (i + 1)]
        turned = pltpu.roll(tile, 64, 1)
        for h in range(2):
            place = places_ref[2 * i + h]
            shard, half = place >> 1, place & 1
            moved = jnp.where(jnp.full((8, 128), half, jnp.int32) == h, tile, turned)
            out_ref[shard] = jnp.where((lane >> 6) == half, moved, out_ref[shard])


def unpack_tile(places_ref, ret_ref, i):
    lane = lax.broadcasted_iota(jnp.int32, (8, 128), 1)
    moved = []
    for h in range(2):
        place = places_ref[2 * i + h]
        shard, half = place >> 1, place & 1
        tile = ret_ref[shard]
        turned = pltpu.roll(tile, 64, 1)
        moved.append(jnp.where(jnp.full((8, 128), half, jnp.int32) == h, tile, turned))
    return jnp.where(lane < 64, moved[0], moved[1])


def packed_terms(jacobian, values, index):
    count = values.shape[1]
    return jnp.concatenate(
        [
            impulse_rows(jacobian, values),
            index.astype(jnp.float32),
            jnp.zeros((1, count), jnp.float32),
        ],
        axis=0,
    )


def pack_kernel(places_ref, jb_ref, y_ref, ib_ref, out_ref):
    pack_rows(places_ref, packed_terms(jb_ref[...], y_ref[...], ib_ref[...]), out_ref)


def scatter_kernel(recv_ref, ja_ref, y_ref, ia_ref, out_ref, near_ref, acc_ref):
    near_ref[...] = impulse_rows(ja_ref[...], y_ref[...])
    acc_ref[...] = jnp.zeros_like(acc_ref)

    def far(i, carry):
        tiles = [recv_ref[WIDE * i + k] for k in range(WIDE)]
        both = jnp.concatenate(tiles, axis=1)
        scatter_chunk(acc_ref, both[0:6], both[6:7].astype(jnp.int32))
        return carry

    lax.fori_loop(0, recv_ref.shape[0] // WIDE, far, 0)

    def near(i, carry):
        at = pl.ds(pl.multiple_of(i * CHUNK, CHUNK), CHUNK)
        scatter_chunk(acc_ref, near_ref[:, at], ia_ref[:, at])
        return carry

    lax.fori_loop(0, ia_ref.shape[1] // CHUNK, near, 0)
    for t in range(24):
        g, half = t // 2, t % 2
        at = slice(128 * half, 128 * half + 128)
        out_ref[t // 3, 8 * (t % 3) : 8 * (t % 3) + 8, :] = (
            acc_ref[8 * g : 8 * g + 8, at] + acc_ref[96 + 8 * g : 104 + 8 * g, at]
        )


def gather_kernel(full_ref, mass_ref, recv_ref, ia_ref, ja_ref, ret_ref, near_ref, tab_ref, va_ref):
    groups = []
    for g in range(12):
        halves = []
        for half in range(2):
            t = 2 * g + half
            at = slice(8 * (t % 3), 8 * (t % 3) + 8)
            halves.append(full_ref[t // 3, at, :] * mass_ref[t // 3, at, :])
        groups.append(jnp.concatenate(halves, axis=1))
    velocities = jnp.concatenate(groups, axis=0)
    high, low = pair(velocities)
    tab_ref[...] = jnp.concatenate([high, low], axis=0).astype(jnp.bfloat16)
    pad = jnp.zeros((2, CHUNK), jnp.float32)

    def far(i, carry):
        tiles = [recv_ref[WIDE * i + k, 6:7, :] for k in range(WIDE)]
        index = jnp.concatenate(tiles, axis=1).astype(jnp.int32)
        rows = jnp.concatenate(gather_chunk(tab_ref[...], index) + [pad], axis=0)
        for k in range(WIDE):
            ret_ref[WIDE * i + k] = rows[:, 128 * k : 128 * (k + 1)]
        return carry

    lax.fori_loop(0, recv_ref.shape[0] // WIDE, far, 0)

    def near(i, carry):
        at = pl.ds(pl.multiple_of(i * CHUNK, CHUNK), CHUNK)
        rows = gather_chunk(tab_ref[...], ia_ref[:, at]) + [pad]
        va_ref[:, at] = jnp.concatenate(rows, axis=0)
        return carry

    lax.fori_loop(0, ia_ref.shape[1] // CHUNK, near, 0)
    near_ref[...] = velocity_rows(ja_ref[...], va_ref[0:6, :])


def gradient_kernel(
    places_ref, ret_ref, near_ref, jb_ref, comp_ref, gap_ref, y_ref, yp_ref, gp_ref,
    g_ref, sums_ref, vb_ref,
):
    count = y_ref.shape[1]
    for i in range(count // 128):
        vb_ref[:, 128 * i : 128 * (i + 1)] = unpack_tile(places_ref, ret_ref, i)
    gradient = (
        near_ref[...]
        + velocity_rows(jb_ref[...], vb_ref[0:6, :])
        + comp_ref[...] * y_ref[...]
        + gap_ref[...]
    )
    g_ref[...] = gradient
    change = y_ref[...] - yp_ref[...]
    slope = gradient - gp_ref[...]
    rows = []
    for square in (change * change, slope * slope):
        row = jnp.sum(square, axis=0, keepdims=True)
        total = row[:, 0:128]
        for i in range(1, count // 128):
            total = total + row[:, 128 * i : 128 * (i + 1)]
        rows.append(total)
    rows.append(jnp.zeros((6, 128), jnp.float32))
    sums_ref[...] = jnp.concatenate(rows, axis=0)


def step_kernel(
    momentum, places_ref, sums_ref, y_ref, g_ref, xp_ref, mu_ref, act_ref, jb_ref, ib_ref,
    x_ref, yn_ref, out_ref,
):
    total = jnp.sum(sums_ref[...], axis=0)
    total = jnp.sum(total, axis=1, keepdims=True)
    stride = jnp.sqrt((total[0:1] + EPS) / (total[1:2] + EPS))
    z = y_ref[...] - stride * g_ref[...]
    mu = mu_ref[...]
    normal, t1, t2 = z[0:1], z[1:2], z[2:3]
    spread = jnp.sqrt(t1 * t1 + t2 * t2 + SMOOTH * SMOOTH)
    sticking = spread <= mu * normal
    separated = mu * spread <= -normal
    cone_normal = (normal + mu * spread) / (1.0 + mu * mu)
    shrink = mu * cone_normal / spread
    active = act_ref[...] == 1
    out_n = jnp.where(sticking, normal, jnp.where(separated, 0.0, cone_normal))
    out_n = jnp.where(active, out_n, jnp.maximum(normal, 0.0))
    rows = [out_n]
    for t in (t1, t2):
        kept = jnp.where(sticking, t, jnp.where(separated, 0.0, shrink * t))
        rows.append(jnp.where(active, kept, 0.0))
    projected = jnp.concatenate(rows, axis=0)
    x_ref[...] = projected
    following = projected + momentum * (projected - xp_ref[...])
    yn_ref[...] = following
    pack_rows(places_ref, packed_terms(jb_ref[...], following, ib_ref[...]), out_ref)


def f32(*shape):
    return jax.ShapeDtypeStruct(shape, jnp.float32)


def on_device(
    jacobian_a,
    jacobian_b,
    warm_start,
    free_gap,
    compliance,
    friction,
    cone_active,
    body_index_a,
    body_index_b,
    block_owner,
    inverse_mass,
    free_velocity,
):
    shards = lax.axis_size(SHARD)
    sharers = lax.axis_size(CONTACT)
    count = warm_start.shape[1]
    places = slot_places(block_owner, 2)
    index_a = body_index_a[None, :]
    index_b = body_index_b[None, :]
    mu = friction[None, :]
    active = cone_active[None, :]
    mass = (
        inverse_mass.reshape(12, 8, 2, 128).transpose(0, 2, 1, 3).reshape(sharers, 24, 128)
    )

    pack = pl.pallas_call(
        pack_kernel,
        out_shape=f32(shards, 8, 128),
        in_specs=[SMEM, VMEM, VMEM, VMEM],
        out_specs=VMEM,
    )
    scatter = pl.pallas_call(
        scatter_kernel,
        out_shape=f32(sharers, 24, 128),
        in_specs=[VMEM] * 4,
        out_specs=VMEM,
        scratch_shapes=[
            pltpu.VMEM((6, count), jnp.float32),
            pltpu.VMEM((12 * ROWS, LANES), jnp.float32),
        ],
    )
    gather = pl.pallas_call(
        gather_kernel,
        out_shape=(f32(shards, 8, 128), f32(3, count)),
        in_specs=[VMEM] * 5,
        out_specs=(VMEM, VMEM),
        scratch_shapes=[
            pltpu.VMEM((12 * ROWS, LANES), jnp.bfloat16),
            pltpu.VMEM((8, count), jnp.float32),
        ],
    )
    gradient_call = pl.pallas_call(
        gradient_kernel,
        out_shape=(f32(3, count), f32(8, 128)),
        in_specs=[SMEM] + [VMEM] * 8,
        out_specs=(VMEM, VMEM),
        scratch_shapes=[pltpu.VMEM((8, count), jnp.float32)],
    )

    def body_impulse(received, values):
        partial = exchange(scatter(received, jacobian_a, values, index_a), CONTACT)
        mine = jnp.sum(partial, axis=0)
        return exchange(jnp.broadcast_to(mine[None], (sharers, *mine.shape)), CONTACT)

    momentum = momentum_table(ITERS)
    current = warm_start
    before = jnp.zeros_like(warm_start)
    gradient_before = free_gap
    latest = warm_start
    packed = pack(places, jacobian_b, warm_start, index_b)
    for rounds in range(ITERS):
        received = exchange(packed, SHARD)
        full = body_impulse(received, current)
        returned, near = gather(full, mass, received, index_a, jacobian_a)
        gradient, sums = gradient_call(
            places, exchange(returned, SHARD), near, jacobian_b, compliance, free_gap,
            current, before, gradient_before,
        )
        sums = exchange(jnp.broadcast_to(sums[None], (sharers, 8, 128)), CONTACT)
        sums = jnp.sum(sums, axis=0)
        sums = exchange(jnp.broadcast_to(sums[None], (shards, 8, 128)), SHARD)
        last = rounds == ITERS - 1
        step = pl.pallas_call(
            lambda *refs, m=0.0 if last else momentum[rounds]: step_kernel(m, *refs),
            out_shape=(f32(3, count), f32(3, count), f32(shards, 8, 128)),
            in_specs=[SMEM] + [VMEM] * 8,
            out_specs=(VMEM, VMEM, VMEM),
        )
        projected, following, packed = step(
            places, sums, current, gradient, latest, mu, active, jacobian_b, index_b
        )
        before, gradient_before, latest, current = current, gradient, projected, following
    full = body_impulse(exchange(packed, SHARD), latest)
    total = full.reshape(12, 2, 8, 128).transpose(0, 2, 1, 3).reshape(inverse_mass.shape)
    velocity = free_velocity + inverse_mass * total
    return (latest, velocity)


def solution(mesh):
    torus = Mesh(
        mesh.devices.reshape(4, 2, mesh.shape["body"], mesh.shape["group"]),
        ("contact_0", "contact_1", "body", "group"),
    )
    placed = (
        P(None, CONTACT_BODY_GROUP),
        P(None, CONTACT_BODY_GROUP),
        P(None, CONTACT_BODY_GROUP),
        P(None, CONTACT_BODY_GROUP),
        P(None, CONTACT_BODY_GROUP),
        P(CONTACT_BODY_GROUP),
        P(CONTACT_BODY_GROUP),
        P(CONTACT_BODY_GROUP),
        P(CONTACT_BODY_GROUP),
        P(CONTACT_BODY_GROUP, None),
        P(None, ("body", "group")),
        P(None, ("body", "group")),
    )
    return jax.shard_map(
        on_device,
        mesh=torus,
        in_specs=placed,
        out_specs=(P(None, CONTACT_BODY_GROUP), P(None, ("body", "group"))),
        check_vma=False,
    )
```

```python
import math

import jax
import jax.numpy as jnp
from jax import lax
from jax.experimental import pallas as pl
from jax.experimental.pallas import tpu as pltpu
from jax.sharding import Mesh
from jax.sharding import PartitionSpec as P

CBLK = 64
ITERS = 2
CONTACT = ("contact_0", "contact_1")
SHARD = ("body", "group")
CONTACT_BODY_GROUP = ("contact_0", "contact_1", "body", "group")

EPS = 1e-06
SMOOTH = 0.1

LANES = 256
ROWS = 16
CHUNK = 512
WIDE = CHUNK // 128

VMEM = pl.BlockSpec(memory_space=pltpu.VMEM)
SMEM = pl.BlockSpec(memory_space=pltpu.SMEM)


def momentum_table(iterations):
    theta_now = 1.0
    coefficients = []
    for rounds in range(iterations):
        following = 0.5 * (
            theta_now * math.sqrt(theta_now * theta_now + 4.0) - theta_now * theta_now
        )
        coefficients.append(theta_now * (1.0 - theta_now) / (theta_now * theta_now + following))
        theta_now = following
    return coefficients


def slot_places(block_owner, capacity):
    target = block_owner[:, 0]
    matching = (target[:, None] == target[None, :]).astype(jnp.int32)
    ordinal = jnp.arange(target.shape[0], dtype=jnp.int32)
    earlier = (ordinal[None, :] < ordinal[:, None]).astype(jnp.int32)
    ranking = jnp.sum(matching * earlier, axis=1)
    return target * capacity + ranking


def impulse_rows(jacobian, values):
    total = jacobian[0:6] * values[0:1]
    for r in range(1, 3):
        total = total + jacobian[6 * r : 6 * r + 6] * values[r : r + 1]
    return total


def velocity_rows(jacobian, velocities):
    rows = [
        jnp.sum(jacobian[6 * r : 6 * r + 6] * velocities, axis=0, keepdims=True)
        for r in range(3)
    ]
    return jnp.concatenate(rows, axis=0)


def lane_onehot(index):
    lane = index & (LANES - 1)
    iota = lax.broadcasted_iota(jnp.int32, (LANES, index.shape[1]), 0)
    return jnp.where(iota == lane, 1.0, 0.0).astype(jnp.bfloat16)


def row_mask(index):
    iota = lax.broadcasted_iota(jnp.int32, (ROWS, index.shape[1]), 0)
    return iota == (index >> 8)


def pair(values):
    high = values.astype(jnp.bfloat16).astype(jnp.float32)
    return high, values - high


def scatter_chunk(acc_ref, terms, index):
    mask = row_mask(index)
    high, low = pair(terms)
    parts = [jnp.where(mask, part[c : c + 1], 0.0) for part in (high, low) for c in range(6)]
    spread = jnp.concatenate(parts, axis=0).astype(jnp.bfloat16)
    acc_ref[...] += lax.dot_general(
        spread,
        lane_onehot(index),
        (((1,), (1,)), ((), ())),
        preferred_element_type=jnp.float32,
    )


def gather_chunk(table, index):
    mask = row_mask(index)
    found = jnp.dot(table, lane_onehot(index), preferred_element_type=jnp.float32)
    found = found[: 6 * ROWS] + found[6 * ROWS :]
    rows = [
        jnp.sum(jnp.where(mask, found[ROWS * c : ROWS * (c + 1)], 0.0), axis=0, keepdims=True)
        for c in range(6)
    ]
    return rows


def pack_rows(places_ref, packed, out_ref):
    out_ref[...] = jnp.zeros_like(out_ref)
    lane = lax.broadcasted_iota(jnp.int32, (8, 128), 1)
    for i in range(packed.shape[1] // 128):
        tile = packed[:, 128 * i : 128 * (i + 1)]
        turned = pltpu.roll(tile, 64, 1)
        for h in range(2):
            place = places_ref[2 * i + h]
            shard, half = place >> 1, place & 1
            moved = jnp.where(jnp.full((8, 128), half, jnp.int32) == h, tile, turned)
            out_ref[shard] = jnp.where((lane >> 6) == half, moved, out_ref[shard])


def unpack_tile(places_ref, ret_ref, i):
    lane = lax.broadcasted_iota(jnp.int32, (8, 128), 1)
    moved = []
    for h in range(2):
        place = places_ref[2 * i + h]
        shard, half = place >> 1, place & 1
        tile = ret_ref[shard]
        turned = pltpu.roll(tile, 64, 1)
        moved.append(jnp.where(jnp.full((8, 128), half, jnp.int32) == h, tile, turned))
    return jnp.where(lane < 64, moved[0], moved[1])


def packed_terms(jacobian, values, index):
    count = values.shape[1]
    return jnp.concatenate(
        [
            impulse_rows(jacobian, values),
            index.astype(jnp.float32),
            jnp.zeros((1, count), jnp.float32),
        ],
        axis=0,
    )


def pack_kernel(places_ref, jb_ref, y_ref, ib_ref, out_ref):
    pack_rows(places_ref, packed_terms(jb_ref[...], y_ref[...], ib_ref[...]), out_ref)


def scatter_kernel(recv_ref, ja_ref, y_ref, ia_ref, out_ref, near_ref, acc_ref):
    near_ref[...] = impulse_rows(ja_ref[...], y_ref[...])
    acc_ref[...] = jnp.zeros_like(acc_ref)

    def far(i, carry):
        tiles = [recv_ref[WIDE * i + k] for k in range(WIDE)]
        both = jnp.concatenate(tiles, axis=1)
        scatter_chunk(acc_ref, both[0:6], both[6:7].astype(jnp.int32))
        return carry

    lax.fori_loop(0, recv_ref.shape[0] // WIDE, far, 0)

    def near(i, carry):
        at = pl.ds(pl.multiple_of(i * CHUNK, CHUNK), CHUNK)
        scatter_chunk(acc_ref, near_ref[:, at], ia_ref[:, at])
        return carry

    lax.fori_loop(0, ia_ref.shape[1] // CHUNK, near, 0)
    for t in range(24):
        g, half = t // 2, t % 2
        at = slice(128 * half, 128 * half + 128)
        out_ref[t // 3, 8 * (t % 3) : 8 * (t % 3) + 8, :] = (
            acc_ref[8 * g : 8 * g + 8, at] + acc_ref[96 + 8 * g : 104 + 8 * g, at]
        )


def gather_kernel(full_ref, mass_ref, recv_ref, ia_ref, ja_ref, ret_ref, near_ref, tab_ref, va_ref):
    groups = []
    for g in range(12):
        halves = []
        for half in range(2):
            t = 2 * g + half
            at = slice(8 * (t % 3), 8 * (t % 3) + 8)
            halves.append(full_ref[t // 3, at, :] * mass_ref[t // 3, at, :])
        groups.append(jnp.concatenate(halves, axis=1))
    velocities = jnp.concatenate(groups, axis=0)
    high, low = pair(velocities)
    tab_ref[...] = jnp.concatenate([high, low], axis=0).astype(jnp.bfloat16)
    pad = jnp.zeros((2, CHUNK), jnp.float32)

    def far(i, carry):
        tiles = [recv_ref[WIDE * i + k, 6:7, :] for k in range(WIDE)]
        index = jnp.concatenate(tiles, axis=1).astype(jnp.int32)
        rows = jnp.concatenate(gather_chunk(tab_ref[...], index) + [pad], axis=0)
        for k in range(WIDE):
            ret_ref[WIDE * i + k] = rows[:, 128 * k : 128 * (k + 1)]
        return carry

    lax.fori_loop(0, recv_ref.shape[0] // WIDE, far, 0)

    def near(i, carry):
        at = pl.ds(pl.multiple_of(i * CHUNK, CHUNK), CHUNK)
        rows = gather_chunk(tab_ref[...], ia_ref[:, at]) + [pad]
        va_ref[:, at] = jnp.concatenate(rows, axis=0)
        return carry

    lax.fori_loop(0, ia_ref.shape[1] // CHUNK, near, 0)
    near_ref[...] = velocity_rows(ja_ref[...], va_ref[0:6, :])


def gradient_kernel(
    places_ref, ret_ref, near_ref, jb_ref, comp_ref, gap_ref, y_ref, yp_ref, gp_ref,
    g_ref, sums_ref, vb_ref,
):
    count = y_ref.shape[1]
    for i in range(count // 128):
        vb_ref[:, 128 * i : 128 * (i + 1)] = unpack_tile(places_ref, ret_ref, i)
    gradient = (
        near_ref[...]
        + velocity_rows(jb_ref[...], vb_ref[0:6, :])
        + comp_ref[...] * y_ref[...]
        + gap_ref[...]
    )
    g_ref[...] = gradient
    change = y_ref[...] - yp_ref[...]
    slope = gradient - gp_ref[...]
    rows = []
    for square in (change * change, slope * slope):
        row = jnp.sum(square, axis=0, keepdims=True)
        total = row[:, 0:128]
        for i in range(1, count // 128):
            total = total + row[:, 128 * i : 128 * (i + 1)]
        rows.append(total)
    rows.append(jnp.zeros((6, 128), jnp.float32))
    sums_ref[...] = jnp.concatenate(rows, axis=0)


def step_kernel(
    momentum, places_ref, sums_ref, y_ref, g_ref, xp_ref, mu_ref, act_ref, jb_ref, ib_ref,
    x_ref, yn_ref, out_ref,
):
    total = jnp.sum(sums_ref[...], axis=1, keepdims=True)
    stride = jnp.sqrt((total[0:1] + EPS) / (total[1:2] + EPS))
    z = y_ref[...] - stride * g_ref[...]
    mu = mu_ref[...]
    normal, t1, t2 = z[0:1], z[1:2], z[2:3]
    spread = jnp.sqrt(t1 * t1 + t2 * t2 + SMOOTH * SMOOTH)
    sticking = spread <= mu * normal
    separated = mu * spread <= -normal
    cone_normal = (normal + mu * spread) / (1.0 + mu * mu)
    shrink = mu * cone_normal / spread
    active = act_ref[...] == 1
    out_n = jnp.where(sticking, normal, jnp.where(separated, 0.0, cone_normal))
    out_n = jnp.where(active, out_n, jnp.maximum(normal, 0.0))
    rows = [out_n]
    for t in (t1, t2):
        kept = jnp.where(sticking, t, jnp.where(separated, 0.0, shrink * t))
        rows.append(jnp.where(active, kept, 0.0))
    projected = jnp.concatenate(rows, axis=0)
    x_ref[...] = projected
    following = projected + momentum * (projected - xp_ref[...])
    yn_ref[...] = following
    pack_rows(places_ref, packed_terms(jb_ref[...], following, ib_ref[...]), out_ref)


def remote(src, dst, send_sem, recv_sem, device_id):
    return pltpu.make_async_remote_copy(
        src_ref=src,
        dst_ref=dst,
        send_sem=send_sem,
        recv_sem=recv_sem,
        device_id=device_id,
        device_id_type=pl.DeviceIdType.MESH,
    )


def contact_id(index):
    return {"contact_0": index // 2, "contact_1": lax.rem(index, 2)}


def greet(ids):
    barrier = pltpu.get_barrier_semaphore()
    for device_id in ids:
        pl.semaphore_signal(
            barrier, inc=1, device_id=device_id, device_id_type=pl.DeviceIdType.MESH
        )
    pl.semaphore_wait(barrier, len(ids))


def trade_kernel(src_ref, dst_ref, send_sem, recv_sem):
    body, group = lax.axis_index("body"), lax.axis_index("group")
    bodies, groups = lax.axis_size("body"), lax.axis_size("group")
    me = body * groups + group

    def to(k):
        return lax.rem(body + k // groups, bodies), lax.rem(group + lax.rem(k, groups), groups)

    def source(k):
        b = lax.rem(body - k // groups + bodies, bodies)
        return b * groups + lax.rem(group - lax.rem(k, groups) + groups, groups)

    def signal(k, carry):
        b, g = to(k)
        pl.semaphore_signal(
            pltpu.get_barrier_semaphore(),
            inc=1,
            device_id={"body": b, "group": g},
            device_id_type=pl.DeviceIdType.MESH,
        )
        return carry

    lax.fori_loop(1, bodies * groups, signal, 0)
    pl.semaphore_wait(pltpu.get_barrier_semaphore(), bodies * groups - 1)

    def send(k, carry):
        b, g = to(k)
        remote(
            src_ref.at[b * groups + g],
            dst_ref.at[me],
            send_sem.at[k],
            recv_sem.at[k],
            {"body": b, "group": g},
        ).start()
        return carry

    lax.fori_loop(1, bodies * groups, send, 0)
    dst_ref[me] = src_ref[me]

    def wait(k, carry):
        b, g = to(k)
        copy = remote(
            src_ref.at[b * groups + g],
            dst_ref.at[source(k)],
            send_sem.at[k],
            recv_sem.at[k],
            {"body": b, "group": g},
        )
        copy.wait_send()
        copy.wait_recv()
        return carry

    lax.fori_loop(1, bodies * groups, wait, 0)


def contact_kernel(part_ref, full_ref, land_ref, mine_ref, send_sem, recv_sem):
    n = part_ref.shape[0]
    me = lax.axis_index("contact_0") * 2 + lax.axis_index("contact_1")
    peers = [lax.rem(me + k, n) for k in range(1, n)]
    greet([contact_id(p) for p in peers])
    copies = []
    for k, p in enumerate(peers):
        copy = remote(
            part_ref.at[p], land_ref.at[k], send_sem.at[0, k], recv_sem.at[0, k], contact_id(p)
        )
        copy.start()
        copies.append(copy)
    total = part_ref[me]
    for k, copy in enumerate(copies):
        copy.wait_recv()
        total = total + land_ref[k]
    mine_ref[...] = total
    full_ref[me] = total
    for k, p in enumerate(peers):
        copy = remote(
            mine_ref, full_ref.at[me], send_sem.at[1, k], recv_sem.at[1, k], contact_id(p)
        )
        copy.start()
        copies.append(copy)
    for k in range(n - 1):
        copies[k].wait_send()
        copies[n - 1 + k].wait_send()
        sender = lax.rem(me - (k + 1) + n, n)
        remote(
            mine_ref,
            full_ref.at[sender],
            send_sem.at[1, k],
            recv_sem.at[1, k],
            contact_id(peers[k]),
        ).wait_recv()


def sums_kernel(sums_ref, out_ref, land_ref, held_ref, send_sem, recv_sem):
    n = land_ref.shape[1]
    axes = (
        (lax.axis_index("contact_0") * 2 + lax.axis_index("contact_1"), contact_id),
        (lax.axis_index("body"), lambda p: {"body": p}),
        (lax.axis_index("group"), lambda p: {"group": p}),
    )
    peers = [[lax.rem(me + k, n) for k in range(1, n)] for me, _ in axes]
    greet([name(p) for (_, name), row in zip(axes, peers) for p in row])
    for a, (me, name) in enumerate(axes):
        src = sums_ref if a == 0 else held_ref.at[a - 1]
        copies = []
        for k, p in enumerate(peers[a]):
            copy = remote(
                src, land_ref.at[a, me], send_sem.at[a, k], recv_sem.at[a, k], name(p)
            )
            copy.start()
            copies.append(copy)
        land_ref[a, me] = src[...]
        for k, p in enumerate(peers[a]):
            copies[k].wait_send()
            sender = lax.rem(me - (k + 1) + n, n)
            remote(
                src, land_ref.at[a, sender], send_sem.at[a, k], recv_sem.at[a, k], name(p)
            ).wait_recv()
        total = land_ref[a, 0]
        for i in range(1, n):
            total = total + land_ref[a, i]
        if a < 2:
            held_ref[a] = total
        else:
            out_ref[...] = total


def f32(*shape):
    return jax.ShapeDtypeStruct(shape, jnp.float32)


def on_device(
    jacobian_a,
    jacobian_b,
    warm_start,
    free_gap,
    compliance,
    friction,
    cone_active,
    body_index_a,
    body_index_b,
    block_owner,
    inverse_mass,
    free_velocity,
):
    shards = lax.axis_size(SHARD)
    sharers = lax.axis_size(CONTACT)
    count = warm_start.shape[1]
    places = slot_places(block_owner, 2)
    index_a = body_index_a[None, :]
    index_b = body_index_b[None, :]
    mu = friction[None, :]
    active = cone_active[None, :]
    mass = (
        inverse_mass.reshape(12, 8, 2, 128).transpose(0, 2, 1, 3).reshape(sharers, 24, 128)
    )

    pack = pl.pallas_call(
        pack_kernel,
        out_shape=f32(shards, 8, 128),
        in_specs=[SMEM, VMEM, VMEM, VMEM],
        out_specs=VMEM,
    )
    scatter = pl.pallas_call(
        scatter_kernel,
        out_shape=f32(sharers, 24, 128),
        in_specs=[VMEM] * 4,
        out_specs=VMEM,
        scratch_shapes=[
            pltpu.VMEM((6, count), jnp.float32),
            pltpu.VMEM((12 * ROWS, LANES), jnp.float32),
        ],
    )
    gather = pl.pallas_call(
        gather_kernel,
        out_shape=(f32(shards, 8, 128), f32(3, count)),
        in_specs=[VMEM] * 5,
        out_specs=(VMEM, VMEM),
        scratch_shapes=[
            pltpu.VMEM((12 * ROWS, LANES), jnp.bfloat16),
            pltpu.VMEM((8, count), jnp.float32),
        ],
    )
    gradient_call = pl.pallas_call(
        gradient_kernel,
        out_shape=(f32(3, count), f32(8, 128)),
        in_specs=[SMEM] + [VMEM] * 8,
        out_specs=(VMEM, VMEM),
        scratch_shapes=[pltpu.VMEM((8, count), jnp.float32)],
    )

    def call(kernel, shape, scratch, number):
        return pl.pallas_call(
            kernel,
            out_shape=shape,
            in_specs=[VMEM],
            out_specs=VMEM,
            scratch_shapes=scratch,
            compiler_params=pltpu.CompilerParams(collective_id=number, has_side_effects=True),
        )

    dma = pltpu.SemaphoreType.DMA
    trade = call(trade_kernel, f32(shards, 8, 128), [dma((shards,)), dma((shards,))], 0)
    share = call(
        contact_kernel,
        f32(sharers, 24, 128),
        [
            pltpu.VMEM((sharers - 1, 24, 128), jnp.float32),
            pltpu.VMEM((24, 128), jnp.float32),
            dma((2, sharers - 1)),
            dma((2, sharers - 1)),
        ],
        1,
    )
    add_up = call(
        sums_kernel,
        f32(8, 128),
        [
            pltpu.VMEM((3, sharers, 8, 128), jnp.float32),
            pltpu.VMEM((2, 8, 128), jnp.float32),
            dma((3, sharers - 1)),
            dma((3, sharers - 1)),
        ],
        2,
    )

    def body_impulse(received, values):
        return share(scatter(received, jacobian_a, values, index_a))

    momentum = momentum_table(ITERS)
    current = warm_start
    before = jnp.zeros_like(warm_start)
    gradient_before = free_gap
    latest = warm_start
    packed = pack(places, jacobian_b, warm_start, index_b)
    for rounds in range(ITERS):
        received = trade(packed)
        full = body_impulse(received, current)
        returned, near = gather(full, mass, received, index_a, jacobian_a)
        gradient, sums = gradient_call(
            places, trade(returned), near, jacobian_b, compliance, free_gap,
            current, before, gradient_before,
        )
        sums = add_up(sums)
        last = rounds == ITERS - 1
        step = pl.pallas_call(
            lambda *refs, m=0.0 if last else momentum[rounds]: step_kernel(m, *refs),
            out_shape=(f32(3, count), f32(3, count), f32(shards, 8, 128)),
            in_specs=[SMEM] + [VMEM] * 8,
            out_specs=(VMEM, VMEM, VMEM),
        )
        projected, following, packed = step(
            places, sums, current, gradient, latest, mu, active, jacobian_b, index_b
        )
        before, gradient_before, latest, current = current, gradient, projected, following
    full = body_impulse(trade(packed), latest)
    total = full.reshape(12, 2, 8, 128).transpose(0, 2, 1, 3).reshape(inverse_mass.shape)
    velocity = free_velocity + inverse_mass * total
    return (latest, velocity)


def solution(mesh):
    torus = Mesh(
        mesh.devices.reshape(4, 2, mesh.shape["body"], mesh.shape["group"]),
        ("contact_0", "contact_1", "body", "group"),
    )
    placed = (
        P(None, CONTACT_BODY_GROUP),
        P(None, CONTACT_BODY_GROUP),
        P(None, CONTACT_BODY_GROUP),
        P(None, CONTACT_BODY_GROUP),
        P(None, CONTACT_BODY_GROUP),
        P(CONTACT_BODY_GROUP),
        P(CONTACT_BODY_GROUP),
        P(CONTACT_BODY_GROUP),
        P(CONTACT_BODY_GROUP),
        P(CONTACT_BODY_GROUP, None),
        P(None, ("body", "group")),
        P(None, ("body", "group")),
    )
    return jax.shard_map(
        on_device,
        mesh=torus,
        in_specs=placed,
        out_specs=(P(None, CONTACT_BODY_GROUP), P(None, ("body", "group"))),
        check_vma=False,
    )
```

```python
import functools
import math

import jax
import jax.numpy as jnp
from jax import lax
from jax.experimental import pallas as pl
from jax.experimental.pallas import tpu as pltpu
from jax.sharding import Mesh
from jax.sharding import PartitionSpec as P

CBLK = 64
ITERS = 2
CONTACT = ("contact_0", "contact_1")
SHARD = ("body", "group")
CONTACT_BODY_GROUP = ("contact_0", "contact_1", "body", "group")

EPS = 1e-06
SMOOTH = 0.1

LANES = 256
ROWS = 16
CHUNK = 512
WIDE = CHUNK // 128

VMEM = pl.BlockSpec(memory_space=pltpu.VMEM)
SMEM = pl.BlockSpec(memory_space=pltpu.SMEM)


def momentum_table(iterations):
    theta_now = 1.0
    coefficients = []
    for rounds in range(iterations):
        following = 0.5 * (
            theta_now * math.sqrt(theta_now * theta_now + 4.0) - theta_now * theta_now
        )
        coefficients.append(theta_now * (1.0 - theta_now) / (theta_now * theta_now + following))
        theta_now = following
    return coefficients


def slot_places(block_owner, capacity):
    target = block_owner[:, 0]
    matching = (target[:, None] == target[None, :]).astype(jnp.int32)
    ordinal = jnp.arange(target.shape[0], dtype=jnp.int32)
    earlier = (ordinal[None, :] < ordinal[:, None]).astype(jnp.int32)
    ranking = jnp.sum(matching * earlier, axis=1)
    return target * capacity + ranking


def impulse_rows(jacobian, values):
    total = jacobian[0:6] * values[0:1]
    for r in range(1, 3):
        total = total + jacobian[6 * r : 6 * r + 6] * values[r : r + 1]
    return total


def velocity_rows(jacobian, velocities):
    rows = [
        jnp.sum(jacobian[6 * r : 6 * r + 6] * velocities, axis=0, keepdims=True)
        for r in range(3)
    ]
    return jnp.concatenate(rows, axis=0)


def lane_onehot(index):
    lane = index & (LANES - 1)
    iota = lax.broadcasted_iota(jnp.int32, (LANES, index.shape[1]), 0)
    return jnp.where(iota == lane, 1.0, 0.0).astype(jnp.bfloat16)


def row_mask(index):
    iota = lax.broadcasted_iota(jnp.int32, (ROWS, index.shape[1]), 0)
    return iota == (index >> 8)


def pair(values):
    high = values.astype(jnp.bfloat16).astype(jnp.float32)
    return high, values - high


def scatter_chunk(acc_ref, terms, index):
    mask = row_mask(index)
    high, low = pair(terms)
    parts = [jnp.where(mask, part[c : c + 1], 0.0) for part in (high, low) for c in range(6)]
    spread = jnp.concatenate(parts, axis=0).astype(jnp.bfloat16)
    acc_ref[...] += lax.dot_general(
        spread,
        lane_onehot(index),
        (((1,), (1,)), ((), ())),
        preferred_element_type=jnp.float32,
    )


def gather_chunk(table, index):
    mask = row_mask(index)
    found = jnp.dot(table, lane_onehot(index), preferred_element_type=jnp.float32)
    found = found[: 6 * ROWS] + found[6 * ROWS :]
    rows = [
        jnp.sum(jnp.where(mask, found[ROWS * c : ROWS * (c + 1)], 0.0), axis=0, keepdims=True)
        for c in range(6)
    ]
    return rows


def pack_rows(places_ref, packed, out_ref):
    out_ref[...] = jnp.zeros_like(out_ref)
    lane = lax.broadcasted_iota(jnp.int32, (8, 128), 1)
    for i in range(packed.shape[1] // 128):
        tile = packed[:, 128 * i : 128 * (i + 1)]
        turned = pltpu.roll(tile, 64, 1)
        for h in range(2):
            place = places_ref[2 * i + h]
            shard, half = place >> 1, place & 1
            moved = jnp.where(jnp.full((8, 128), half, jnp.int32) == h, tile, turned)
            out_ref[shard] = jnp.where((lane >> 6) == half, moved, out_ref[shard])


def unpack_tile(places_ref, ret_ref, i):
    lane = lax.broadcasted_iota(jnp.int32, (8, 128), 1)
    moved = []
    for h in range(2):
        place = places_ref[2 * i + h]
        shard, half = place >> 1, place & 1
        tile = ret_ref[shard]
        turned = pltpu.roll(tile, 64, 1)
        moved.append(jnp.where(jnp.full((8, 128), half, jnp.int32) == h, tile, turned))
    return jnp.where(lane < 64, moved[0], moved[1])


def packed_terms(jacobian, values, index):
    count = values.shape[1]
    return jnp.concatenate(
        [
            impulse_rows(jacobian, values),
            index.astype(jnp.float32),
            jnp.zeros((1, count), jnp.float32),
        ],
        axis=0,
    )


def pack_kernel(places_ref, jb_ref, y_ref, ib_ref, out_ref):
    pack_rows(places_ref, packed_terms(jb_ref[...], y_ref[...], ib_ref[...]), out_ref)


def gradient_kernel(
    places_ref, ret_ref, near_ref, jb_ref, comp_ref, gap_ref, y_ref, yp_ref, gp_ref,
    g_ref, sums_ref, vb_ref,
):
    count = y_ref.shape[1]
    for i in range(count // 128):
        vb_ref[:, 128 * i : 128 * (i + 1)] = unpack_tile(places_ref, ret_ref, i)
    gradient = (
        near_ref[...]
        + velocity_rows(jb_ref[...], vb_ref[0:6, :])
        + comp_ref[...] * y_ref[...]
        + gap_ref[...]
    )
    g_ref[...] = gradient
    change = y_ref[...] - yp_ref[...]
    slope = gradient - gp_ref[...]
    rows = []
    for square in (change * change, slope * slope):
        row = jnp.sum(square, axis=0, keepdims=True)
        total = row[:, 0:128]
        for i in range(1, count // 128):
            total = total + row[:, 128 * i : 128 * (i + 1)]
        rows.append(total)
    rows.append(jnp.zeros((6, 128), jnp.float32))
    sums_ref[...] = jnp.concatenate(rows, axis=0)


def step_kernel(
    momentum, places_ref, sums_ref, y_ref, g_ref, xp_ref, mu_ref, act_ref, jb_ref, ib_ref,
    x_ref, yn_ref, out_ref,
):
    total = jnp.sum(sums_ref[...], axis=1, keepdims=True)
    stride = jnp.sqrt((total[0:1] + EPS) / (total[1:2] + EPS))
    z = y_ref[...] - stride * g_ref[...]
    mu = mu_ref[...]
    normal, t1, t2 = z[0:1], z[1:2], z[2:3]
    spread = jnp.sqrt(t1 * t1 + t2 * t2 + SMOOTH * SMOOTH)
    sticking = spread <= mu * normal
    separated = mu * spread <= -normal
    cone_normal = (normal + mu * spread) / (1.0 + mu * mu)
    shrink = mu * cone_normal / spread
    active = act_ref[...] == 1
    out_n = jnp.where(sticking, normal, jnp.where(separated, 0.0, cone_normal))
    out_n = jnp.where(active, out_n, jnp.maximum(normal, 0.0))
    rows = [out_n]
    for t in (t1, t2):
        kept = jnp.where(sticking, t, jnp.where(separated, 0.0, shrink * t))
        rows.append(jnp.where(active, kept, 0.0))
    projected = jnp.concatenate(rows, axis=0)
    x_ref[...] = projected
    following = projected + momentum * (projected - xp_ref[...])
    yn_ref[...] = following
    pack_rows(places_ref, packed_terms(jb_ref[...], following, ib_ref[...]), out_ref)


def remote(src, dst, send_sem, recv_sem, device_id):
    return pltpu.make_async_remote_copy(
        src_ref=src,
        dst_ref=dst,
        send_sem=send_sem,
        recv_sem=recv_sem,
        device_id=device_id,
        device_id_type=pl.DeviceIdType.MESH,
    )


def contact_id(index):
    return {"contact_0": index // 2, "contact_1": lax.rem(index, 2)}


def signal(device_id):
    pl.semaphore_signal(
        pltpu.get_barrier_semaphore(),
        inc=1,
        device_id=device_id,
        device_id_type=pl.DeviceIdType.MESH,
    )


def middle_kernel(final, packed_ref, mass_ref, ja_ref, y_ref, ia_ref, *refs):
    outs = 1 if final else 2
    (recv_ref, near_ref, acc_ref, part_ref, land_ref, mine_ref, go_send, go_recv, c_send, c_recv) = (
        refs[outs : outs + 10]
    )
    if final:
        full_ref = refs[0]
    else:
        ret_ref, nearv_ref = refs[:2]
        full_ref, back_ref, tab_ref, va_ref, back_send, back_recv = refs[outs + 10 :]
    body, group = lax.axis_index("body"), lax.axis_index("group")
    bodies, groups = lax.axis_size("body"), lax.axis_size("group")
    shards = bodies * groups
    me = body * groups + group
    n = part_ref.shape[0]
    mine = lax.axis_index("contact_0") * 2 + lax.axis_index("contact_1")
    peers = [lax.rem(mine + k, n) for k in range(1, n)]

    def to(k):
        return lax.rem(body + k // groups, bodies), lax.rem(group + lax.rem(k, groups), groups)

    def source(k):
        b = lax.rem(body - k // groups + bodies, bodies)
        return b, lax.rem(group - lax.rem(k, groups) + groups, groups)

    def name(b, g):
        return {"body": b, "group": g}

    def going(k):
        b, g = to(k)
        at = b * groups + g
        return remote(packed_ref.at[at], recv_ref.at[k], go_send.at[k], go_recv.at[k], name(b, g))

    def backing(k):
        b, g = source(k)
        return remote(back_ref.at[k], ret_ref.at[me], back_send.at[k], back_recv.at[k], name(b, g))

    def loop(low, high, act):
        def turn(k, carry):
            act(k)
            return carry

        lax.fori_loop(low, high, turn, 0)

    loop(1, shards, lambda k: signal(name(*to(k))))
    for p in peers:
        signal(contact_id(p))

    near_ref[...] = impulse_rows(ja_ref[...], y_ref[...])
    acc_ref[...] = jnp.zeros_like(acc_ref)

    def near(i):
        at = pl.ds(pl.multiple_of(i * CHUNK, CHUNK), CHUNK)
        scatter_chunk(acc_ref, near_ref[:, at], ia_ref[:, at])

    loop(0, ia_ref.shape[1] // CHUNK, near)
    pl.semaphore_wait(pltpu.get_barrier_semaphore(), shards - 1 + n - 1)

    loop(1, shards, lambda k: going(k).start())
    recv_ref[0] = packed_ref[me]

    def far(i, first=0):
        for k in range(first, WIDE):
            going(WIDE * i + k).wait_recv()
        both = jnp.concatenate([recv_ref[WIDE * i + k] for k in range(WIDE)], axis=1)
        scatter_chunk(acc_ref, both[0:6], both[6:7].astype(jnp.int32))

    far(0, 1)
    loop(1, shards // WIDE, far)

    for t in range(24):
        g, half = t // 2, t % 2
        at = slice(128 * half, 128 * half + 128)
        part_ref[t // 3, 8 * (t % 3) : 8 * (t % 3) + 8, :] = (
            acc_ref[8 * g : 8 * g + 8, at] + acc_ref[96 + 8 * g : 104 + 8 * g, at]
        )
    loop(1, shards, lambda k: going(k).wait_send())
    copies = []
    for k, p in enumerate(peers):
        copy = remote(
            part_ref.at[p], land_ref.at[k], c_send.at[0, k], c_recv.at[0, k], contact_id(p)
        )
        copy.start()
        copies.append(copy)
    total = part_ref[mine]
    for k, copy in enumerate(copies):
        copy.wait_recv()
        total = total + land_ref[k]
    mine_ref[...] = total
    full_ref[mine] = total
    for k, p in enumerate(peers):
        copy = remote(
            mine_ref, full_ref.at[mine], c_send.at[1, k], c_recv.at[1, k], contact_id(p)
        )
        copy.start()
        copies.append(copy)
    for k in range(n - 1):
        copies[k].wait_send()
        copies[n - 1 + k].wait_send()
        sender = lax.rem(mine - (k + 1) + n, n)
        remote(
            mine_ref,
            full_ref.at[sender],
            c_send.at[1, k],
            c_recv.at[1, k],
            contact_id(peers[k]),
        ).wait_recv()
    if final:
        return

    rows = []
    for g in range(12):
        halves = []
        for t in (2 * g, 2 * g + 1):
            at = slice(8 * (t % 3), 8 * (t % 3) + 8)
            halves.append(full_ref[t // 3, at, :] * mass_ref[t // 3, at, :])
        rows.append(jnp.concatenate(halves, axis=1))
    high, low = pair(jnp.concatenate(rows, axis=0))
    tab_ref[...] = jnp.concatenate([high, low], axis=0).astype(jnp.bfloat16)
    pad = jnp.zeros((2, CHUNK), jnp.float32)

    def find(i):
        tiles = [recv_ref[WIDE * i + k, 6:7, :] for k in range(WIDE)]
        index = jnp.concatenate(tiles, axis=1).astype(jnp.int32)
        found = jnp.concatenate(gather_chunk(tab_ref[...], index) + [pad], axis=0)
        for k in range(WIDE):
            back_ref[WIDE * i + k] = found[:, 128 * k : 128 * (k + 1)]

    def give(i, first=0):
        for k in range(first, WIDE):
            backing(WIDE * i + k).start()

    find(0)
    find(1)
    give(0, 1)

    def find_give(i):
        find(i)
        give(i - 1)

    loop(2, shards // WIDE, find_give)
    ret_ref[me] = back_ref[0]
    give(shards // WIDE - 1)

    def near_find(i):
        at = pl.ds(pl.multiple_of(i * CHUNK, CHUNK), CHUNK)
        va_ref[:, at] = jnp.concatenate(gather_chunk(tab_ref[...], ia_ref[:, at]) + [pad], axis=0)

    loop(0, ia_ref.shape[1] // CHUNK, near_find)
    nearv_ref[...] = velocity_rows(ja_ref[...], va_ref[0:6, :])

    def finish(k):
        backing(k).wait_send()
        b, g = to(k)
        remote(
            back_ref.at[k],
            ret_ref.at[b * groups + g],
            back_send.at[k],
            back_recv.at[k],
            name(b, g),
        ).wait_recv()

    loop(1, shards, finish)


def sums_kernel(sums_ref, out_ref, land_ref, held_ref, send_sem, recv_sem):
    n = land_ref.shape[1]
    axes = (
        (lax.axis_index("contact_0") * 2 + lax.axis_index("contact_1"), contact_id),
        (lax.axis_index("body"), lambda p: {"body": p}),
        (lax.axis_index("group"), lambda p: {"group": p}),
    )
    peers = [[lax.rem(me + k, n) for k in range(1, n)] for me, _ in axes]
    for (_, name), row in zip(axes, peers):
        for p in row:
            signal(name(p))
    pl.semaphore_wait(pltpu.get_barrier_semaphore(), 3 * (n - 1))
    for a, (me, name) in enumerate(axes):
        src = sums_ref if a == 0 else held_ref.at[a - 1]
        copies = []
        for k, p in enumerate(peers[a]):
            copy = remote(
                src, land_ref.at[a, me], send_sem.at[a, k], recv_sem.at[a, k], name(p)
            )
            copy.start()
            copies.append(copy)
        land_ref[a, me] = src[...]
        for k, p in enumerate(peers[a]):
            copies[k].wait_send()
            sender = lax.rem(me - (k + 1) + n, n)
            remote(
                src, land_ref.at[a, sender], send_sem.at[a, k], recv_sem.at[a, k], name(p)
            ).wait_recv()
        total = land_ref[a, 0]
        for i in range(1, n):
            total = total + land_ref[a, i]
        if a < 2:
            held_ref[a] = total
        else:
            out_ref[...] = total


def f32(*shape):
    return jax.ShapeDtypeStruct(shape, jnp.float32)


def on_device(
    jacobian_a,
    jacobian_b,
    warm_start,
    free_gap,
    compliance,
    friction,
    cone_active,
    body_index_a,
    body_index_b,
    block_owner,
    inverse_mass,
    free_velocity,
):
    shards = lax.axis_size(SHARD)
    sharers = lax.axis_size(CONTACT)
    count = warm_start.shape[1]
    places = slot_places(block_owner, 2)
    index_a = body_index_a[None, :]
    index_b = body_index_b[None, :]
    mu = friction[None, :]
    active = cone_active[None, :]
    mass = (
        inverse_mass.reshape(12, 8, 2, 128).transpose(0, 2, 1, 3).reshape(sharers, 24, 128)
    )

    pack = pl.pallas_call(
        pack_kernel,
        out_shape=f32(shards, 8, 128),
        in_specs=[SMEM, VMEM, VMEM, VMEM],
        out_specs=VMEM,
    )
    gradient_call = pl.pallas_call(
        gradient_kernel,
        out_shape=(f32(3, count), f32(8, 128)),
        in_specs=[SMEM] + [VMEM] * 8,
        out_specs=(VMEM, VMEM),
        scratch_shapes=[pltpu.VMEM((8, count), jnp.float32)],
    )

    dma = pltpu.SemaphoreType.DMA

    def call(kernel, operands, shape, scratch, number):
        return pl.pallas_call(
            kernel,
            out_shape=shape,
            in_specs=[VMEM] * operands,
            out_specs=jax.tree.map(lambda _: VMEM, shape),
            scratch_shapes=scratch,
            compiler_params=pltpu.CompilerParams(collective_id=number, has_side_effects=True),
        )

    def space(*shape):
        return pltpu.VMEM(shape, jnp.float32)

    common = [
        space(shards, 8, 128),
        space(6, count),
        space(12 * ROWS, LANES),
        space(sharers, 24, 128),
        space(sharers - 1, 24, 128),
        space(24, 128),
        dma((shards,)),
        dma((shards,)),
        dma((2, sharers - 1)),
        dma((2, sharers - 1)),
    ]
    middle = call(
        functools.partial(middle_kernel, False),
        5,
        (f32(shards, 8, 128), f32(3, count)),
        common
        + [
            space(sharers, 24, 128),
            space(shards, 8, 128),
            pltpu.VMEM((12 * ROWS, LANES), jnp.bfloat16),
            space(8, count),
            dma((shards,)),
            dma((shards,)),
        ],
        0,
    )
    ending = call(
        functools.partial(middle_kernel, True), 5, f32(sharers, 24, 128), common, 1
    )
    add_up = call(
        sums_kernel,
        1,
        f32(8, 128),
        [
            space(3, sharers, 8, 128),
            space(2, 8, 128),
            dma((3, sharers - 1)),
            dma((3, sharers - 1)),
        ],
        2,
    )

    momentum = momentum_table(ITERS)
    current = warm_start
    before = jnp.zeros_like(warm_start)
    gradient_before = free_gap
    latest = warm_start
    packed = pack(places, jacobian_b, warm_start, index_b)
    for rounds in range(ITERS):
        returned, near = middle(packed, mass, jacobian_a, current, index_a)
        gradient, sums = gradient_call(
            places, returned, near, jacobian_b, compliance, free_gap,
            current, before, gradient_before,
        )
        sums = add_up(sums)
        last = rounds == ITERS - 1
        step = pl.pallas_call(
            lambda *refs, m=0.0 if last else momentum[rounds]: step_kernel(m, *refs),
            out_shape=(f32(3, count), f32(3, count), f32(shards, 8, 128)),
            in_specs=[SMEM] + [VMEM] * 8,
            out_specs=(VMEM, VMEM, VMEM),
        )
        projected, following, packed = step(
            places, sums, current, gradient, latest, mu, active, jacobian_b, index_b
        )
        before, gradient_before, latest, current = current, gradient, projected, following
    full = ending(packed, mass, jacobian_a, latest, index_a)
    total = full.reshape(12, 2, 8, 128).transpose(0, 2, 1, 3).reshape(inverse_mass.shape)
    velocity = free_velocity + inverse_mass * total
    return (latest, velocity)


def solution(mesh):
    torus = Mesh(
        mesh.devices.reshape(4, 2, mesh.shape["body"], mesh.shape["group"]),
        ("contact_0", "contact_1", "body", "group"),
    )
    placed = (
        P(None, CONTACT_BODY_GROUP),
        P(None, CONTACT_BODY_GROUP),
        P(None, CONTACT_BODY_GROUP),
        P(None, CONTACT_BODY_GROUP),
        P(None, CONTACT_BODY_GROUP),
        P(CONTACT_BODY_GROUP),
        P(CONTACT_BODY_GROUP),
        P(CONTACT_BODY_GROUP),
        P(CONTACT_BODY_GROUP),
        P(CONTACT_BODY_GROUP, None),
        P(None, ("body", "group")),
        P(None, ("body", "group")),
    )
    return jax.shard_map(
        on_device,
        mesh=torus,
        in_specs=placed,
        out_specs=(P(None, CONTACT_BODY_GROUP), P(None, ("body", "group"))),
        check_vma=False,
    )
```

```python
import functools
import math

import jax
import jax.numpy as jnp
from jax import lax
from jax.experimental import pallas as pl
from jax.experimental.pallas import tpu as pltpu
from jax.sharding import Mesh
from jax.sharding import PartitionSpec as P

CBLK = 64
ITERS = 2
CONTACT = ("contact_0", "contact_1")
SHARD = ("body", "group")
CONTACT_BODY_GROUP = ("contact_0", "contact_1", "body", "group")

EPS = 1e-06
SMOOTH = 0.1

LANES = 256
ROWS = 16
CHUNK = 512
WIDE = CHUNK // 128

VMEM = pl.BlockSpec(memory_space=pltpu.VMEM)
SMEM = pl.BlockSpec(memory_space=pltpu.SMEM)


def momentum_table(iterations):
    theta_now = 1.0
    coefficients = []
    for rounds in range(iterations):
        following = 0.5 * (
            theta_now * math.sqrt(theta_now * theta_now + 4.0) - theta_now * theta_now
        )
        coefficients.append(theta_now * (1.0 - theta_now) / (theta_now * theta_now + following))
        theta_now = following
    return coefficients


def slot_places(block_owner, capacity):
    target = block_owner[:, 0]
    matching = (target[:, None] == target[None, :]).astype(jnp.int32)
    ordinal = jnp.arange(target.shape[0], dtype=jnp.int32)
    earlier = (ordinal[None, :] < ordinal[:, None]).astype(jnp.int32)
    ranking = jnp.sum(matching * earlier, axis=1)
    return target * capacity + ranking


def impulse_rows(jacobian, values):
    total = jacobian[0:6] * values[0:1]
    for r in range(1, 3):
        total = total + jacobian[6 * r : 6 * r + 6] * values[r : r + 1]
    return total


def velocity_rows(jacobian, velocities):
    rows = [
        jnp.sum(jacobian[6 * r : 6 * r + 6] * velocities, axis=0, keepdims=True)
        for r in range(3)
    ]
    return jnp.concatenate(rows, axis=0)


def lane_onehot(index):
    lane = index & (LANES - 1)
    iota = lax.broadcasted_iota(jnp.int32, (LANES, index.shape[1]), 0)
    return jnp.where(iota == lane, 1.0, 0.0).astype(jnp.bfloat16)


def row_mask(index):
    iota = lax.broadcasted_iota(jnp.int32, (ROWS, index.shape[1]), 0)
    return iota == (index >> 8)


def pair(values):
    high = values.astype(jnp.bfloat16).astype(jnp.float32)
    return high, values - high


def scatter_chunk(acc_ref, terms, index):
    mask = row_mask(index)
    high, low = pair(terms)
    parts = [jnp.where(mask, part[c : c + 1], 0.0) for part in (high, low) for c in range(6)]
    spread = jnp.concatenate(parts, axis=0).astype(jnp.bfloat16)
    acc_ref[...] += lax.dot_general(
        spread,
        lane_onehot(index),
        (((1,), (1,)), ((), ())),
        preferred_element_type=jnp.float32,
    )


def gather_chunk(table, index):
    mask = row_mask(index)
    found = jnp.dot(table, lane_onehot(index), preferred_element_type=jnp.float32)
    found = found[: 6 * ROWS] + found[6 * ROWS :]
    rows = [
        jnp.sum(jnp.where(mask, found[ROWS * c : ROWS * (c + 1)], 0.0), axis=0, keepdims=True)
        for c in range(6)
    ]
    return rows


def pack_rows(places_ref, packed, out_ref):
    out_ref[...] = jnp.zeros_like(out_ref)
    lane = lax.broadcasted_iota(jnp.int32, (8, 128), 1)
    for i in range(packed.shape[1] // 128):
        tile = packed[:, 128 * i : 128 * (i + 1)]
        turned = pltpu.roll(tile, 64, 1)
        for h in range(2):
            place = places_ref[2 * i + h]
            shard, half = place >> 1, place & 1
            moved = jnp.where(jnp.full((8, 128), half, jnp.int32) == h, tile, turned)
            out_ref[shard] = jnp.where((lane >> 6) == half, moved, out_ref[shard])


def unpack_tile(places_ref, ret_ref, i):
    lane = lax.broadcasted_iota(jnp.int32, (8, 128), 1)
    moved = []
    for h in range(2):
        place = places_ref[2 * i + h]
        shard, half = place >> 1, place & 1
        tile = ret_ref[shard]
        turned = pltpu.roll(tile, 64, 1)
        moved.append(jnp.where(jnp.full((8, 128), half, jnp.int32) == h, tile, turned))
    return jnp.where(lane < 64, moved[0], moved[1])


def packed_terms(jacobian, values, index):
    count = values.shape[1]
    return jnp.concatenate(
        [
            impulse_rows(jacobian, values),
            index.astype(jnp.float32),
            jnp.zeros((1, count), jnp.float32),
        ],
        axis=0,
    )


def pack_kernel(places_ref, jb_ref, y_ref, ib_ref, out_ref):
    pack_rows(places_ref, packed_terms(jb_ref[...], y_ref[...], ib_ref[...]), out_ref)


def gradient_kernel(
    places_ref, ret_ref, near_ref, jb_ref, comp_ref, gap_ref, y_ref, yp_ref, gp_ref,
    g_ref, sums_ref, vb_ref,
):
    count = y_ref.shape[1]
    for i in range(count // 128):
        vb_ref[:, 128 * i : 128 * (i + 1)] = unpack_tile(places_ref, ret_ref, i)
    gradient = (
        near_ref[...]
        + velocity_rows(jb_ref[...], vb_ref[0:6, :])
        + comp_ref[...] * y_ref[...]
        + gap_ref[...]
    )
    g_ref[...] = gradient
    change = y_ref[...] - yp_ref[...]
    slope = gradient - gp_ref[...]
    rows = []
    for square in (change * change, slope * slope):
        row = jnp.sum(square, axis=0, keepdims=True)
        total = row[:, 0:128]
        for i in range(1, count // 128):
            total = total + row[:, 128 * i : 128 * (i + 1)]
        rows.append(total)
    rows.append(jnp.zeros((6, 128), jnp.float32))
    sums_ref[...] = jnp.concatenate(rows, axis=0)


def step_kernel(
    momentum, places_ref, sums_ref, y_ref, g_ref, xp_ref, mu_ref, act_ref, jb_ref, ib_ref,
    x_ref, yn_ref, out_ref,
):
    total = jnp.sum(sums_ref[...], axis=1, keepdims=True)
    stride = jnp.sqrt((total[0:1] + EPS) / (total[1:2] + EPS))
    z = y_ref[...] - stride * g_ref[...]
    mu = mu_ref[...]
    normal, t1, t2 = z[0:1], z[1:2], z[2:3]
    spread = jnp.sqrt(t1 * t1 + t2 * t2 + SMOOTH * SMOOTH)
    sticking = spread <= mu * normal
    separated = mu * spread <= -normal
    cone_normal = (normal + mu * spread) / (1.0 + mu * mu)
    shrink = mu * cone_normal / spread
    active = act_ref[...] == 1
    out_n = jnp.where(sticking, normal, jnp.where(separated, 0.0, cone_normal))
    out_n = jnp.where(active, out_n, jnp.maximum(normal, 0.0))
    rows = [out_n]
    for t in (t1, t2):
        kept = jnp.where(sticking, t, jnp.where(separated, 0.0, shrink * t))
        rows.append(jnp.where(active, kept, 0.0))
    projected = jnp.concatenate(rows, axis=0)
    x_ref[...] = projected
    following = projected + momentum * (projected - xp_ref[...])
    yn_ref[...] = following
    pack_rows(places_ref, packed_terms(jb_ref[...], following, ib_ref[...]), out_ref)


def remote(src, dst, send_sem, recv_sem, device_id):
    return pltpu.make_async_remote_copy(
        src_ref=src,
        dst_ref=dst,
        send_sem=send_sem,
        recv_sem=recv_sem,
        device_id=device_id,
        device_id_type=pl.DeviceIdType.MESH,
    )


def contact_id(index):
    return {"contact_0": index // 2, "contact_1": lax.rem(index, 2)}


def signal(device_id):
    pl.semaphore_signal(
        pltpu.get_barrier_semaphore(),
        inc=1,
        device_id=device_id,
        device_id_type=pl.DeviceIdType.MESH,
    )


def middle_kernel(final, packed_ref, mass_ref, ja_ref, y_ref, ia_ref, *refs):
    outs = 1 if final else 2
    (recv_ref, near_ref, acc_ref, part_ref, land_ref, mine_ref, go_send, go_recv, c_send, c_recv) = (
        refs[outs : outs + 10]
    )
    if final:
        full_ref = refs[0]
    else:
        ret_ref, nearv_ref = refs[:2]
        full_ref, back_ref, tab_ref, va_ref, back_send, back_recv = refs[outs + 10 :]
    body, group = lax.axis_index("body"), lax.axis_index("group")
    bodies, groups = lax.axis_size("body"), lax.axis_size("group")
    shards = bodies * groups
    me = body * groups + group
    n = part_ref.shape[0]
    mine = lax.axis_index("contact_0") * 2 + lax.axis_index("contact_1")
    peers = [lax.rem(mine + k, n) for k in range(1, n)]

    def offset(i, n):
        far = (i + 1) // 2
        return lax.rem(far * (1 - 2 * lax.rem(i + 1, 2)) + n, n)

    def to(k):
        b = offset(k // groups, bodies)
        g = offset(lax.rem(k, groups), groups)
        return lax.rem(body + b, bodies), lax.rem(group + g, groups)

    def source(k):
        b = offset(k // groups, bodies)
        g = offset(lax.rem(k, groups), groups)
        return lax.rem(body - b + bodies, bodies), lax.rem(group - g + groups, groups)

    def name(b, g):
        return {"body": b, "group": g}

    def going(k):
        b, g = to(k)
        at = b * groups + g
        return remote(packed_ref.at[at], recv_ref.at[k], go_send.at[k], go_recv.at[k], name(b, g))

    def backing(k):
        b, g = source(k)
        return remote(back_ref.at[k], ret_ref.at[me], back_send.at[k], back_recv.at[k], name(b, g))

    def loop(low, high, act):
        def turn(k, carry):
            act(k)
            return carry

        lax.fori_loop(low, high, turn, 0)

    loop(1, shards, lambda k: signal(name(*to(shards - k))))
    for p in peers:
        signal(contact_id(p))

    near_ref[...] = impulse_rows(ja_ref[...], y_ref[...])
    acc_ref[...] = jnp.zeros_like(acc_ref)

    def near(i):
        at = pl.ds(pl.multiple_of(i * CHUNK, CHUNK), CHUNK)
        scatter_chunk(acc_ref, near_ref[:, at], ia_ref[:, at])

    loop(0, ia_ref.shape[1] // CHUNK, near)
    pl.semaphore_wait(pltpu.get_barrier_semaphore(), shards - 1 + n - 1)

    loop(1, shards, lambda k: going(shards - k).start())
    recv_ref[0] = packed_ref[me]

    def far(i, first=0):
        for k in range(first, WIDE):
            going(WIDE * i + k).wait_recv()
        both = jnp.concatenate([recv_ref[WIDE * i + k] for k in range(WIDE)], axis=1)
        scatter_chunk(acc_ref, both[0:6], both[6:7].astype(jnp.int32))

    far(0, 1)
    loop(1, shards // WIDE, far)

    for t in range(24):
        g, half = t // 2, t % 2
        at = slice(128 * half, 128 * half + 128)
        part_ref[t // 3, 8 * (t % 3) : 8 * (t % 3) + 8, :] = (
            acc_ref[8 * g : 8 * g + 8, at] + acc_ref[96 + 8 * g : 104 + 8 * g, at]
        )
    loop(1, shards, lambda k: going(k).wait_send())
    copies = []
    for k, p in enumerate(peers):
        copy = remote(
            part_ref.at[p], land_ref.at[k], c_send.at[0, k], c_recv.at[0, k], contact_id(p)
        )
        copy.start()
        copies.append(copy)
    total = part_ref[mine]
    for k, copy in enumerate(copies):
        copy.wait_recv()
        total = total + land_ref[k]
    mine_ref[...] = total
    full_ref[mine] = total
    for k, p in enumerate(peers):
        copy = remote(
            mine_ref, full_ref.at[mine], c_send.at[1, k], c_recv.at[1, k], contact_id(p)
        )
        copy.start()
        copies.append(copy)
    for k in range(n - 1):
        copies[k].wait_send()
        copies[n - 1 + k].wait_send()
        sender = lax.rem(mine - (k + 1) + n, n)
        remote(
            mine_ref,
            full_ref.at[sender],
            c_send.at[1, k],
            c_recv.at[1, k],
            contact_id(peers[k]),
        ).wait_recv()
    if final:
        return

    rows = []
    for g in range(12):
        halves = []
        for t in (2 * g, 2 * g + 1):
            at = slice(8 * (t % 3), 8 * (t % 3) + 8)
            halves.append(full_ref[t // 3, at, :] * mass_ref[t // 3, at, :])
        rows.append(jnp.concatenate(halves, axis=1))
    high, low = pair(jnp.concatenate(rows, axis=0))
    tab_ref[...] = jnp.concatenate([high, low], axis=0).astype(jnp.bfloat16)
    pad = jnp.zeros((2, CHUNK), jnp.float32)

    def find(i):
        tiles = [recv_ref[WIDE * i + k, 6:7, :] for k in range(WIDE)]
        index = jnp.concatenate(tiles, axis=1).astype(jnp.int32)
        found = jnp.concatenate(gather_chunk(tab_ref[...], index) + [pad], axis=0)
        for k in range(WIDE):
            back_ref[WIDE * i + k] = found[:, 128 * k : 128 * (k + 1)]

    def give(i, first=0):
        for k in range(first, WIDE):
            backing(WIDE * i + k).start()

    last = shards // WIDE - 1
    find(last)

    def find_give(i):
        find(last - i)
        give(last - i + 1)

    loop(1, last + 1, find_give)
    ret_ref[me] = back_ref[0]
    give(0, 1)

    def near_find(i):
        at = pl.ds(pl.multiple_of(i * CHUNK, CHUNK), CHUNK)
        va_ref[:, at] = jnp.concatenate(gather_chunk(tab_ref[...], ia_ref[:, at]) + [pad], axis=0)

    loop(0, ia_ref.shape[1] // CHUNK, near_find)
    nearv_ref[...] = velocity_rows(ja_ref[...], va_ref[0:6, :])

    def finish(k):
        backing(k).wait_send()
        b, g = to(k)
        remote(
            back_ref.at[k],
            ret_ref.at[b * groups + g],
            back_send.at[k],
            back_recv.at[k],
            name(b, g),
        ).wait_recv()

    loop(1, shards, finish)


def sums_kernel(sums_ref, out_ref, land_ref, held_ref, send_sem, recv_sem):
    n = land_ref.shape[1]
    axes = (
        (lax.axis_index("contact_0") * 2 + lax.axis_index("contact_1"), contact_id),
        (lax.axis_index("body"), lambda p: {"body": p}),
        (lax.axis_index("group"), lambda p: {"group": p}),
    )
    peers = [[lax.rem(me + k, n) for k in range(1, n)] for me, _ in axes]
    for (_, name), row in zip(axes, peers):
        for p in row:
            signal(name(p))
    pl.semaphore_wait(pltpu.get_barrier_semaphore(), 3 * (n - 1))
    for a, (me, name) in enumerate(axes):
        src = sums_ref if a == 0 else held_ref.at[a - 1]
        copies = []
        for k, p in enumerate(peers[a]):
            copy = remote(
                src, land_ref.at[a, me], send_sem.at[a, k], recv_sem.at[a, k], name(p)
            )
            copy.start()
            copies.append(copy)
        land_ref[a, me] = src[...]
        for k, p in enumerate(peers[a]):
            copies[k].wait_send()
            sender = lax.rem(me - (k + 1) + n, n)
            remote(
                src, land_ref.at[a, sender], send_sem.at[a, k], recv_sem.at[a, k], name(p)
            ).wait_recv()
        total = land_ref[a, 0]
        for i in range(1, n):
            total = total + land_ref[a, i]
        if a < 2:
            held_ref[a] = total
        else:
            out_ref[...] = total


def f32(*shape):
    return jax.ShapeDtypeStruct(shape, jnp.float32)


def on_device(
    jacobian_a,
    jacobian_b,
    warm_start,
    free_gap,
    compliance,
    friction,
    cone_active,
    body_index_a,
    body_index_b,
    block_owner,
    inverse_mass,
    free_velocity,
):
    shards = lax.axis_size(SHARD)
    sharers = lax.axis_size(CONTACT)
    count = warm_start.shape[1]
    places = slot_places(block_owner, 2)
    index_a = body_index_a[None, :]
    index_b = body_index_b[None, :]
    mu = friction[None, :]
    active = cone_active[None, :]
    mass = (
        inverse_mass.reshape(12, 8, 2, 128).transpose(0, 2, 1, 3).reshape(sharers, 24, 128)
    )

    pack = pl.pallas_call(
        pack_kernel,
        out_shape=f32(shards, 8, 128),
        in_specs=[SMEM, VMEM, VMEM, VMEM],
        out_specs=VMEM,
    )
    gradient_call = pl.pallas_call(
        gradient_kernel,
        out_shape=(f32(3, count), f32(8, 128)),
        in_specs=[SMEM] + [VMEM] * 8,
        out_specs=(VMEM, VMEM),
        scratch_shapes=[pltpu.VMEM((8, count), jnp.float32)],
    )

    dma = pltpu.SemaphoreType.DMA

    def call(kernel, operands, shape, scratch, number):
        return pl.pallas_call(
            kernel,
            out_shape=shape,
            in_specs=[VMEM] * operands,
            out_specs=jax.tree.map(lambda _: VMEM, shape),
            scratch_shapes=scratch,
            compiler_params=pltpu.CompilerParams(collective_id=number, has_side_effects=True),
        )

    def space(*shape):
        return pltpu.VMEM(shape, jnp.float32)

    common = [
        space(shards, 8, 128),
        space(6, count),
        space(12 * ROWS, LANES),
        space(sharers, 24, 128),
        space(sharers - 1, 24, 128),
        space(24, 128),
        dma((shards,)),
        dma((shards,)),
        dma((2, sharers - 1)),
        dma((2, sharers - 1)),
    ]
    middle = call(
        functools.partial(middle_kernel, False),
        5,
        (f32(shards, 8, 128), f32(3, count)),
        common
        + [
            space(sharers, 24, 128),
            space(shards, 8, 128),
            pltpu.VMEM((12 * ROWS, LANES), jnp.bfloat16),
            space(8, count),
            dma((shards,)),
            dma((shards,)),
        ],
        0,
    )
    ending = call(
        functools.partial(middle_kernel, True), 5, f32(sharers, 24, 128), common, 1
    )
    add_up = call(
        sums_kernel,
        1,
        f32(8, 128),
        [
            space(3, sharers, 8, 128),
            space(2, 8, 128),
            dma((3, sharers - 1)),
            dma((3, sharers - 1)),
        ],
        2,
    )

    momentum = momentum_table(ITERS)
    current = warm_start
    before = jnp.zeros_like(warm_start)
    gradient_before = free_gap
    latest = warm_start
    packed = pack(places, jacobian_b, warm_start, index_b)
    for rounds in range(ITERS):
        returned, near = middle(packed, mass, jacobian_a, current, index_a)
        gradient, sums = gradient_call(
            places, returned, near, jacobian_b, compliance, free_gap,
            current, before, gradient_before,
        )
        sums = add_up(sums)
        last = rounds == ITERS - 1
        step = pl.pallas_call(
            lambda *refs, m=0.0 if last else momentum[rounds]: step_kernel(m, *refs),
            out_shape=(f32(3, count), f32(3, count), f32(shards, 8, 128)),
            in_specs=[SMEM] + [VMEM] * 8,
            out_specs=(VMEM, VMEM, VMEM),
        )
        projected, following, packed = step(
            places, sums, current, gradient, latest, mu, active, jacobian_b, index_b
        )
        before, gradient_before, latest, current = current, gradient, projected, following
    full = ending(packed, mass, jacobian_a, latest, index_a)
    total = full.reshape(12, 2, 8, 128).transpose(0, 2, 1, 3).reshape(inverse_mass.shape)
    velocity = free_velocity + inverse_mass * total
    return (latest, velocity)


def solution(mesh):
    torus = Mesh(
        mesh.devices.reshape(4, 2, mesh.shape["body"], mesh.shape["group"]),
        ("contact_0", "contact_1", "body", "group"),
    )
    placed = (
        P(None, CONTACT_BODY_GROUP),
        P(None, CONTACT_BODY_GROUP),
        P(None, CONTACT_BODY_GROUP),
        P(None, CONTACT_BODY_GROUP),
        P(None, CONTACT_BODY_GROUP),
        P(CONTACT_BODY_GROUP),
        P(CONTACT_BODY_GROUP),
        P(CONTACT_BODY_GROUP),
        P(CONTACT_BODY_GROUP),
        P(CONTACT_BODY_GROUP, None),
        P(None, ("body", "group")),
        P(None, ("body", "group")),
    )
    return jax.shard_map(
        on_device,
        mesh=torus,
        in_specs=placed,
        out_specs=(P(None, CONTACT_BODY_GROUP), P(None, ("body", "group"))),
        check_vma=False,
    )
```
